1024 devices in a mesh: gx: 16 (over z, core), gy: 64 (over y, x).
Axes of the slice: x: 8, y: 8, z: 8, core: 2. Of those that a mesh axis runs over, the one named last changes fastest.
Arguments:
- particles: float32 [12288, 6, 128], P(('gx', 'gy')), may hold values from -6 to 6
- occupancy: int32 [12288], P(('gx', 'gy')), may hold values from 32 to 128, as said below
- neighbours: int32 [12288, 16], P(('gx', 'gy')), may hold values from 0 to 12287, as said below
- curve_cuts: int32 [2, 1024], replicated, may hold values from 0 to 12282, as said below
Outputs:
- after_first: float32 [24576, 6, 128], P(('gx', 'gy'))
- after_second: float32 [24576, 6, 128], P(('gx', 'gy'))
The draws below stay inside these ranges and needn't reach their ends.
Inputs may be any that keep to these rules, and one draw needn't show every extreme that they name: `occupancy`: each tile holds at least 32 live particles, and some tile in every draw holds 128. `neighbours`: tile t lists 16 different tiles among the curve positions t + 1 to t + 24, counted modulo 12288. `curve_cuts`: entry d of each row is d * 12 + e with e between -6 and 6, and e is 0 for device 0; so each device owns 0 to 24 tiles, and in every step some device owns exactly 24.
All inputs are finite; a program needn't handle non-finite values.
Results may differ from the reference program's by a relative error of at most 0.0001.
Values sent between devices are 32-bit elements; how exact they have to be, the bound alone decides.
A program may use at most 32 MiB of HBM per device.

```python
import jax
import jax.numpy as jnp
from jax import lax

TILE_P = 128
NBR = 16
STEPS = 2
TILE_DEV = 12
HALF = 6
CAP = 24
WIN = 24
NT = 12288
DEVICES = 1024


def draw_occupancy(key, part):
    count_key, pick_key = jax.random.split(key)
    filled = jax.random.randint(count_key, (NT,), TILE_P // 4, TILE_P + 1, dtype=jnp.int32)
    chosen = jax.random.randint(pick_key, (), 0, NT, dtype=jnp.int32)
    return filled.at[chosen].set(TILE_P)


def draw_neighbours(key, part):
    scores = jax.random.randint(key, (NT, WIN), 0, 2 ** 20, dtype=jnp.int32) * WIN + jnp.arange(WIN, dtype=jnp.int32)[None, :]
    ranked = jnp.argsort(scores, axis=1, stable=True)[:, :NBR].astype(jnp.int32)
    return ((jnp.arange(NT, dtype=jnp.int32)[:, None] + ranked + 1) % NT).astype(jnp.int32)


def draw_curve_cuts(key, part):
    shift_key, pick_key = jax.random.split(key)
    departure = jax.random.randint(shift_key, (STEPS, DEVICES), -HALF, HALF + 1, dtype=jnp.int32)
    departure = departure.at[:, 0].set(0)
    chosen = jax.random.randint(pick_key, (STEPS,), 1, DEVICES - 1, dtype=jnp.int32)
    step_rows = jnp.arange(STEPS, dtype=jnp.int32)
    departure = departure.at[step_rows, chosen].set(-HALF)
    departure = departure.at[step_rows, chosen + 1].set(HALF)
    return (jnp.arange(DEVICES, dtype=jnp.int32)[None, :] * TILE_DEV + departure).astype(jnp.int32)


def shard_levels(own_key, dims, shards, least, top_value):
    def one(dim, parts):
        steps = jax.random.uniform(jax.random.fold_in(jax.random.fold_in(own_key, 6), dim), (parts,), jnp.float32, least / len(shards), top_value / len(shards))
        return jnp.repeat(jnp.exp(steps), dims[dim] // parts).reshape((-1,) + (1,) * (len(dims) - dim - 1))

    factor_of = one(*shards[0])
    for cut in shards[1:]:
        factor_of = factor_of * one(*cut)
    return factor_of


def noise(own_key, extent, spread, most, shards=(), held_as=jnp.bfloat16):
    values = jax.random.normal(own_key, extent, jnp.float32) * spread
    if len(shards) > 0:
        values = shard_levels(own_key, extent, shards, -0.22, 0.18) * values
    return jnp.clip(values, min=-most, max=most).astype(held_as)


def setup_inputs(seed: int = 0) -> dict:
    streams_of = jax.random.split(jax.random.key(seed), 5)
    particles = noise(streams_of[0], (NT, 6, TILE_P), 1.0, 6.0, ((0, 1024),), jnp.float32)
    occupancy = draw_occupancy(jax.random.fold_in(streams_of[4], 71), 0)
    neighbours = draw_neighbours(jax.random.fold_in(streams_of[4], 71), 0)
    curve_cuts = draw_curve_cuts(jax.random.fold_in(streams_of[4], 71), 0)
    return dict(particles=particles, occupancy=occupancy, neighbours=neighbours, curve_cuts=curve_cuts)


soften = 0.05
time_step = 0.5
block_tiles = 4


def pair_terms(targets, sources):
    target_pos = targets[:, None, :3, :, None]
    source_pos = sources[:, :, :3, None, :]
    separation = source_pos - target_pos
    distance_sq = jnp.sum(separation * separation, axis=2) + soften
    kernel = distance_sq ** -1.5
    action = jnp.sum(kernel[:, :, None] * sources[:, :, 3][:, :, None, None, :] * separation, axis=(1, 4))
    reaction = -jnp.sum(kernel[:, :, None] * targets[:, 3][:, None, None, :, None] * separation, axis=3)
    return action, reaction


def forces(pos_weight, neighbours):
    block_count = NT // block_tiles

    def block_pass(react_pool, inputs):
        targets, source_ids = inputs
        sources = jnp.concatenate([targets[:, None], pos_weight[source_ids]], axis=1)
        action, reaction = pair_terms(targets, sources)
        react_pool = react_pool.at[source_ids.reshape(-1)].add(reaction[:, 1:].reshape(-1, 3, TILE_P))
        return react_pool, action

    start_pool = jnp.zeros((NT, 3, TILE_P), jnp.float32)
    react_pool, actions = lax.scan(block_pass, start_pool, (pos_weight.reshape(block_count, block_tiles, 4, TILE_P), neighbours.reshape(block_count, block_tiles, NBR)))
    return react_pool + actions.reshape(NT, 3, TILE_P)


def reference(particles, occupancy, neighbours, curve_cuts):
    weight = (jnp.arange(TILE_P, dtype=jnp.int32)[None, :] < occupancy[:, None]).astype(jnp.float32)
    position = particles[:, :3]
    velocity = particles[:, 3:]
    snapshots = []
    for step_index in range(STEPS):
        pos_weight = jnp.concatenate([position, weight[:, None]], axis=1)
        acceleration = forces(pos_weight, neighbours)
        velocity = weight[:, None] * (velocity + time_step * acceleration / TILE_P)
        position = weight[:, None] * (position + time_step * velocity)
        starts = curve_cuts[step_index]
        segment_end = jnp.concatenate([starts[1:], jnp.array([NT], jnp.int32)])
        slot_tiles = starts[:, None] + jnp.arange(CAP, dtype=jnp.int32)[None, :]
        occupied = (slot_tiles < segment_end[:, None]).reshape(-1).astype(jnp.float32)
        merged = jnp.concatenate([position, velocity], axis=1)
        picked = merged[jnp.clip(slot_tiles, 0, NT - 1).reshape(-1)]
        snapshots.append(picked * occupied[:, None, None])
    return (snapshots[0], snapshots[1])
```

```python
import functools

import jax
import jax.numpy as jnp
from jax import lax
from jax.experimental import pallas as pl
from jax.experimental.pallas import tpu as pltpu
from jax.sharding import PartitionSpec as P

STEPS = 2
soften = 0.05
time_step = 0.5

MESH = pl.DeviceIdType.MESH
F32 = jnp.float32
BF16 = jnp.bfloat16


def split_rows(rows):
    high = rows.astype(BF16)
    rest = rows - high.astype(F32)
    middle = rest.astype(BF16)
    low = rest - middle.astype(F32)
    return jnp.concatenate(
        [high.astype(F32), low, middle.astype(F32), jnp.zeros_like(low)], axis=0
    ).astype(BF16)


def fold(terms):
    return terms[:4] + terms[4:]


def kernel(
    dims, meta, part, first_out, second_out,
    first_pool, second_pool, terms, columns, self_act, act, react_all, react_out, react_in,
    rows_out, first_window, second_window, send, recv,
):
    outer, inner, tiles, listed, half = dims
    pools = (first_pool, second_pool)
    windows = (first_window, second_window)
    size = outer * inner
    reach = 2 * tiles
    slots = part.shape[2]
    zero_slot = tiles * listed
    inverse_at = tiles * listed
    occupancy_at = inverse_at + tiles * reach
    cuts_at = occupancy_at + tiles
    me = lax.axis_index("gx") * inner + lax.axis_index("gy")

    def device(distance):
        index = (me + distance + size) % size
        return (index // inner, index % inner)

    barrier = pltpu.get_barrier_semaphore()
    for distance in (-2, -1, 1, 2):
        pl.semaphore_signal(barrier, inc=1, device_id=device(distance), device_id_type=MESH)

    lanes = lax.broadcasted_iota(jnp.int32, (1, slots), 1)

    def weight_of(tile):
        return jnp.where(lanes < meta[occupancy_at + tile], 1.0, 0.0).astype(F32)

    for tile in range(tiles):
        first_pool[tile] = jnp.concatenate([part[tile, 0:3], weight_of(tile)], axis=0)
    react_all[zero_slot] = jnp.zeros((8, slots), F32)

    def remote(source, target, slot, distance):
        return pltpu.make_async_remote_copy(
            src_ref=source,
            dst_ref=target,
            send_sem=send.at[slot],
            recv_sem=recv.at[slot],
            device_id=device(distance),
            device_id_type=MESH,
        )

    def position_copies(step):
        return [
            remote(
                pools[step].at[pl.ds(0, tiles)],
                pools[step].at[pl.ds(tiles * distance, tiles)],
                6 * step + distance - 1,
                -distance,
            )
            for distance in (1, 2)
        ]

    def reaction_copies(step):
        return [
            remote(
                react_out.at[step, distance - 1],
                react_in.at[step, distance - 1],
                6 * step + 1 + distance,
                distance,
            )
            for distance in (1, 2)
        ]

    def window_copies(step):
        return [
            remote(
                rows_out.at[step, pl.ds(0, half)],
                windows[step].at[pl.ds(half + tiles, half)],
                6 * step + 4,
                -1,
            ),
            remote(
                rows_out.at[step, pl.ds(tiles - half, half)],
                windows[step].at[pl.ds(0, half)],
                6 * step + 5,
                1,
            ),
        ]

    def prepare(step, tile):
        rows = pools[step][tile]
        terms[tile] = split_rows(rows * rows[3:4])

    def pair(step, tile, source):
        rows = pools[step][source]
        dx = rows[0:1] - columns[tile, 0]
        dy = rows[1:2] - columns[tile, 1]
        dz = rows[2:3] - columns[tile, 2]
        root = lax.rsqrt(dx * dx + (dy * dy + (dz * dz + soften)))
        value = root * root * root
        high = value.astype(BF16)
        low = (value - high.astype(F32)).astype(BF16)
        return high, low

    def action_of(high, low, source):
        rows = terms[source]
        return lax.dot_general(
            jnp.concatenate([high, low], axis=1),
            jnp.concatenate([rows, rows], axis=1),
            (((1,), (1,)), ((), ())),
            preferred_element_type=F32,
        )

    def own_tile(step, tile):
        prepare(step, tile)
        rows = pools[step][tile]
        turned = jnp.transpose(jnp.concatenate([rows, rows], axis=0))
        for axis in range(3):
            columns[tile, axis] = jnp.broadcast_to(turned[:, axis : axis + 1], (slots, slots))
        high, low = pair(step, tile, tile)
        self_act[tile] = action_of(high, low, tile)

    def main_tile(step, tile):
        own = terms[tile]
        own_terms = jnp.concatenate([own, own], axis=1)
        total = self_act[tile]
        for entry in range(listed):
            source = meta[tile * listed + entry]
            high, low = pair(step, tile, source)
            total = total + action_of(high, low, source)
            reaction = jnp.dot(
                own_terms, jnp.concatenate([high, low], axis=0), preferred_element_type=F32
            )
            react_all[tile * listed + entry] = reaction[:8] + reaction[8:]
        turned = jnp.transpose(total)
        act[tile] = turned[:8] + turned[8:]

    def reactions_on(source):
        total = None
        for tile in range(max(0, source - reach), min(tiles, source)):
            entry = react_all[meta[inverse_at + tile * reach + source - tile - 1]]
            total = entry if total is None else total + entry
        return total

    for step in range(STEPS):
        if step == 0:
            pl.semaphore_wait(barrier, 4)
        positions = position_copies(step)
        for copy in positions:
            copy.start()

        lax.fori_loop(
            0, tiles, lambda tile, carry: (own_tile(step, tile), carry)[1], 0, unroll=4
        )
        for distance in (1, 2):
            positions[distance - 1].wait_recv()
            lax.fori_loop(
                tiles * distance,
                tiles * (distance + 1),
                lambda tile, carry: (prepare(step, tile), carry)[1],
                0,
                unroll=4,
            )
        lax.fori_loop(0, tiles, lambda tile, carry: (main_tile(step, tile), carry)[1], 0)

        reactions = reaction_copies(step)
        for distance in (2, 1):
            for tile in range(tiles):
                react_out[step, distance - 1, tile] = fold(
                    reactions_on(tiles * distance + tile)
                )
            reactions[distance - 1].start()
        for tile in range(1, tiles):
            act[tile] = act[tile] + reactions_on(tile)
        for distance in (1, 2):
            reactions[distance - 1].wait_recv()

        for tile in range(tiles):
            total = fold(act[tile]) + react_in[step, 0, tile] + react_in[step, 1, tile]
            rows = pools[step][tile]
            place, weight = rows[0:3], rows[3:4]
            speed = part[tile, 3:6] if step == 0 else rows_out[step - 1, tile, 3:6]
            acceleration = total[0:3] - place * total[3:4]
            speed = weight * (speed + (time_step / slots) * acceleration)
            place = weight * (place + time_step * speed)
            if step + 1 < STEPS:
                pools[step + 1][tile] = jnp.concatenate([place, weight], axis=0)
            rows_out[step, tile] = jnp.concatenate([place, speed], axis=0)
            windows[step][half + tile] = jnp.concatenate([place, speed], axis=0)
        for copy in window_copies(step):
            copy.start()

    for step, out in enumerate((first_out, second_out)):
        for copy in window_copies(step):
            copy.wait_recv()
        begin = meta[cuts_at + 2 * step]
        count = meta[cuts_at + 2 * step + 1]
        for slot in range(2 * tiles):
            rows = windows[step][jnp.minimum(begin + slot, 2 * tiles - 1)]
            out[slot] = jnp.where(slot < count, rows, 0.0)
    for step in range(STEPS):
        for copy in position_copies(step) + reaction_copies(step) + window_copies(step):
            copy.wait_send()


def body(outer, inner, particles, occupancy, neighbours, curve_cuts):
    tiles, fields, slots = particles.shape
    listed = neighbours.shape[1]
    size = outer * inner
    total = size * tiles
    reach = 2 * tiles
    half = tiles // 2
    me = lax.axis_index(("gx", "gy"))
    first = me * tiles
    local = (neighbours - first) % total
    tile_ids = jnp.arange(tiles, dtype=jnp.int32)
    entry_ids = jnp.arange(tiles * listed, dtype=jnp.int32).reshape(tiles, listed)
    offsets = jnp.arange(1, reach + 1, dtype=jnp.int32)
    hit = (local - tile_ids[:, None])[:, None, :] == offsets[None, :, None]
    none = tiles * listed
    inverse = none + jnp.sum(jnp.where(hit, entry_ids[:, None, :] - none, 0), axis=2)
    starts = curve_cuts[:, me]
    ends = jnp.where(me + 1 < size, curve_cuts[:, jnp.minimum(me + 1, size - 1)], total)
    cuts = jnp.stack([starts - (first - half), ends - starts], axis=1)
    meta = jnp.concatenate(
        [local.reshape(-1), inverse.reshape(-1), occupancy, cuts.reshape(-1)]
    ).astype(jnp.int32)
    out_type = jax.ShapeDtypeStruct((2 * tiles, fields, slots), F32)
    vmem = pl.BlockSpec(memory_space=pltpu.VMEM)
    return pl.pallas_call(
        functools.partial(kernel, (outer, inner, tiles, listed, half)),
        out_shape=(out_type, out_type),
        in_specs=[pl.BlockSpec(memory_space=pltpu.SMEM), vmem],
        out_specs=(vmem, vmem),
        scratch_shapes=[
            pltpu.VMEM((3 * tiles, 4, slots), F32),
            pltpu.VMEM((3 * tiles, 4, slots), F32),
            pltpu.VMEM((3 * tiles, 16, slots), BF16),
            pltpu.VMEM((tiles, 3, slots, slots), F32),
            pltpu.VMEM((tiles, slots, 16), F32),
            pltpu.VMEM((tiles, 8, slots), F32),
            pltpu.VMEM((tiles * listed + 1, 8, slots), F32),
            pltpu.VMEM((STEPS, 2, tiles, 4, slots), F32),
            pltpu.VMEM((STEPS, 2, tiles, 4, slots), F32),
            pltpu.VMEM((STEPS, tiles, fields, slots), F32),
            pltpu.VMEM((2 * tiles, fields, slots), F32),
            pltpu.VMEM((2 * tiles, fields, slots), F32),
            pltpu.SemaphoreType.DMA((6 * STEPS,)),
            pltpu.SemaphoreType.DMA((6 * STEPS,)),
        ],
        compiler_params=pltpu.CompilerParams(
            collective_id=0, has_side_effects=True, vmem_limit_bytes=40 << 20
        ),
    )(meta, particles)


def solution(mesh):
    in_specs = (P(("gx", "gy"), None, None), P(("gx", "gy")), P(("gx", "gy"), None), P())
    out_specs = (P(("gx", "gy"), None, None), P(("gx", "gy"), None, None))
    per_device = functools.partial(body, mesh.shape["gx"], mesh.shape["gy"])
    return jax.shard_map(
        per_device, mesh=mesh, in_specs=in_specs, out_specs=out_specs, check_vma=False
    )
```

```python
import functools

import jax
import jax.numpy as jnp
from jax import lax
from jax.experimental import pallas as pl
from jax.experimental.pallas import tpu as pltpu
from jax.sharding import PartitionSpec as P

STEPS = 2
soften = 0.05
time_step = 0.5

MESH = pl.DeviceIdType.MESH
F32 = jnp.float32
BF16 = jnp.bfloat16


def split_rows(rows):
    high = rows.astype(BF16)
    rest = rows - high.astype(F32)
    middle = rest.astype(BF16)
    low = rest - middle.astype(F32)
    return jnp.concatenate(
        [high.astype(F32), low, middle.astype(F32), jnp.zeros_like(low)], axis=0
    ).astype(BF16)


def fold(terms):
    return terms[:4] + terms[4:]


def kernel(
    dims, neighbours, inverse, occupancy, cuts, part, first_out, second_out,
    first_pool, second_pool, speeds, state, terms, columns, self_act, act, react_all,
    partial, from_next, from_second_next, from_last, from_second_last,
    end_last, end_next, end_second_last, end_third_last, first_window, second_window,
    send, recv,
):
    outer, inner, tiles, listed, half = dims
    pools = (first_pool, second_pool)
    size = outer * inner
    total_tiles = size * tiles
    reach = 2 * tiles
    slots = part.shape[2]
    zero_slot = tiles * listed
    me = lax.axis_index("gx") * inner + lax.axis_index("gy")
    first = me * tiles

    def device(distance):
        index = (me + distance + size) % size
        return (index // inner, index % inner)

    barrier = pltpu.get_barrier_semaphore()
    for distance in (-1, 1, -2, 2, -3, 3):
        pl.semaphore_signal(barrier, inc=1, device_id=device(distance), device_id_type=MESH)

    lanes = lax.broadcasted_iota(jnp.int32, (1, slots), 1)
    empty = jnp.zeros((1, slots), F32)
    for tile in range(tiles):
        weight = jnp.where(lanes < occupancy[tile], 1.0, 0.0).astype(F32)
        first_pool[tile] = jnp.concatenate([part[tile, 0:3], weight], axis=0)
        speeds[tile] = jnp.concatenate([part[tile, 3:6], empty], axis=0)
    react_all[zero_slot] = jnp.zeros((8, slots), F32)

    def remote(source, target, slot, distance):
        return pltpu.make_async_remote_copy(
            src_ref=source,
            dst_ref=target,
            send_sem=send.at[slot],
            recv_sem=recv.at[slot],
            device_id=device(distance),
            device_id_type=MESH,
        )

    def tile_copies(buffer, slot):
        return [
            remote(
                buffer.at[pl.ds(0, tiles)],
                buffer.at[pl.ds(tiles * distance, tiles)],
                slot + distance - 1,
                -distance,
            )
            for distance in (1, 2)
        ]

    def rows_copy(step, begin, count, target, slot, distance):
        return remote(partial.at[step, pl.ds(begin, count)], target, slot, distance)

    positions = tile_copies(first_pool, 0)
    motions = tile_copies(speeds, 2)
    mid = [
        rows_copy(0, tiles, 2 * tiles, from_last, 4, 1),
        rows_copy(0, 2 * tiles, tiles, from_second_last, 5, 2),
        rows_copy(0, 0, tiles, from_second_next, 6, -2),
        rows_copy(0, 0, 2 * tiles, from_next, 7, -1),
    ]
    border = remote(
        state.at[pl.ds(tiles - half, half)], state.at[pl.ds(3 * tiles, half)], 8, 1
    )
    end = [
        rows_copy(1, 2 * tiles + half, half, end_third_last, 9, 3),
        rows_copy(1, tiles + half, tiles + half, end_second_last, 10, 2),
        rows_copy(1, half, 2 * tiles, end_last, 11, 1),
        rows_copy(1, 0, half, end_next, 12, -1),
    ]

    def over(begin, end, function, unroll):
        def trip(tile, carry):
            function(tile)
            return carry

        lax.fori_loop(begin, end, trip, 0, unroll=unroll)

    def prepare(rows, tile):
        terms[tile] = split_rows(rows * rows[3:4])

    def pair(step, tile, source):
        rows = pools[step][source]
        dx = rows[0:1] - columns[tile, 0]
        dy = rows[1:2] - columns[tile, 1]
        dz = rows[2:3] - columns[tile, 2]
        root = lax.rsqrt(dx * dx + (dy * dy + (dz * dz + soften)))
        value = root * root * root
        high = value.astype(BF16)
        low = (value - high.astype(F32)).astype(BF16)
        return high, low

    def action_of(high, low, source):
        rows = terms[source]
        return lax.dot_general(
            jnp.concatenate([high, low], axis=1),
            jnp.concatenate([rows, rows], axis=1),
            (((1,), (1,)), ((), ())),
            preferred_element_type=F32,
        )

    def own_tile(step, tile):
        rows = pools[step][tile]
        prepare(rows, tile)
        turned = jnp.transpose(jnp.concatenate([rows, rows], axis=0))
        for axis in range(3):
            columns[tile, axis] = jnp.broadcast_to(turned[:, axis : axis + 1], (slots, slots))
        high, low = pair(step, tile, tile)
        self_act[tile] = action_of(high, low, tile)

    def main_tile(step, tile):
        own = terms[tile]
        own_terms = jnp.concatenate([own, own], axis=1)
        total = self_act[tile]
        for entry in range(listed):
            source = jnp.minimum(
                lax.rem(neighbours[tile, entry] - first + total_tiles, total_tiles),
                3 * tiles - 1,
            )
            high, low = pair(step, tile, source)
            total = total + action_of(high, low, source)
            reaction = jnp.dot(
                own_terms, jnp.concatenate([high, low], axis=0), preferred_element_type=F32
            )
            react_all[tile * listed + entry] = reaction[:8] + reaction[8:]
        turned = jnp.transpose(total)
        act[tile] = turned[:8] + turned[8:]

    def reactions_on(source):
        total = None
        for tile in range(max(0, source - reach), min(tiles, source)):
            entry = react_all[inverse[tile, source - tile - 1]]
            total = entry if total is None else total + entry
        return total

    def moved(place, speed, weight, total):
        acceleration = total[0:3] - place * total[3:4]
        speed = weight * (speed + (time_step / slots) * acceleration)
        place = weight * (place + time_step * speed)
        return place, speed

    pl.semaphore_wait(barrier, 6)
    for copy in positions + motions:
        copy.start()
    over(0, tiles, lambda tile: own_tile(0, tile), 4)
    for distance in (1, 2):
        positions[distance - 1].wait_recv()
        over(
            tiles * distance,
            tiles * (distance + 1),
            lambda tile: prepare(first_pool[tile], tile),
            4,
        )
    over(0, tiles, lambda tile: main_tile(0, tile), 1)

    for tile in range(2 * tiles, 3 * tiles):
        partial[0, tile] = fold(reactions_on(tile))
    mid[1].start()
    for tile in range(tiles, 2 * tiles):
        partial[0, tile] = fold(reactions_on(tile))
    mid[0].start()
    for tile in range(tiles):
        total = act[tile] if tile == 0 else act[tile] + reactions_on(tile)
        partial[0, tile] = fold(total)
    mid[2].start()
    mid[3].start()

    def first_update(tile, total):
        rows, speed = first_pool[tile], speeds[tile]
        place, speed = moved(rows[0:3], speed[0:3], rows[3:4], total)
        second_pool[tile] = jnp.concatenate([place, rows[3:4]], axis=0)
        state[tile] = jnp.concatenate([place, speed, rows[3:4], empty], axis=0)

    mid[0].wait_recv()
    mid[1].wait_recv()
    over(
        0,
        tiles,
        lambda tile: first_update(
            tile, partial[0, tile] + from_last[tile] + from_second_last[tile]
        ),
        4,
    )
    border.start()
    over(0, tiles, lambda tile: own_tile(1, tile), 4)
    motions[0].wait_recv()
    motions[1].wait_recv()
    mid[3].wait_recv()

    def next_update(tile):
        first_update(
            tiles + tile, from_next[tile] + partial[0, tiles + tile] + from_last[tiles + tile]
        )
        prepare(second_pool[tiles + tile], tiles + tile)

    over(0, tiles, next_update, 4)
    mid[2].wait_recv()

    def second_next_update(tile):
        first_update(
            2 * tiles + tile,
            from_second_next[tile] + from_next[tiles + tile] + partial[0, 2 * tiles + tile],
        )
        prepare(second_pool[2 * tiles + tile], 2 * tiles + tile)

    over(0, tiles, second_next_update, 4)
    over(0, tiles, lambda tile: main_tile(1, tile), 1)

    for tile in range(2 * tiles, 3 * tiles):
        partial[1, tile] = fold(reactions_on(tile))
    end[0].start()
    for tile in range(tiles, 2 * tiles):
        partial[1, tile] = fold(reactions_on(tile))
    end[1].start()
    for tile in range(tiles):
        total = act[tile] if tile == 0 else act[tile] + reactions_on(tile)
        partial[1, tile] = fold(total)
    end[2].start()
    end[3].start()

    border.wait_recv()
    for tile in range(half):
        first_window[tile] = state[3 * tiles + tile, 0:6]
    for tile in range(tiles + half):
        first_window[half + tile] = state[tile, 0:6]

    def place_slots(step, window, out):
        begin = cuts[step, me] - (first - half)
        following = cuts[step, jnp.minimum(me + 1, size - 1)]
        count = jnp.where(me + 1 < size, following, total_tiles) - cuts[step, me]
        for slot in range(2 * tiles):
            rows = window[jnp.clip(begin + slot, 0, 2 * tiles - 1)]
            out[slot] = jnp.where(slot < count, rows, 0.0)

    place_slots(0, first_window, first_out)

    def second_update(tile, slot, total):
        rows = state[tile]
        place, speed = moved(rows[0:3], rows[3:6], rows[6:7], total)
        second_window[slot] = jnp.concatenate([place, speed], axis=0)

    end[2].wait_recv()
    end[1].wait_recv()
    for tile in range(tiles):
        second_update(
            tile,
            half + tile,
            partial[1, tile] + end_last[half + tile] + end_second_last[half + tile],
        )
    end[3].wait_recv()
    for tile in range(half):
        second_update(
            tiles + tile,
            half + tiles + tile,
            end_next[tile] + partial[1, tiles + tile] + end_last[tiles + half + tile],
        )
    end[0].wait_recv()
    for tile in range(half):
        second_update(
            3 * tiles + tile, tile, end_last[tile] + end_second_last[tile] + end_third_last[tile]
        )
    place_slots(1, second_window, second_out)
    for copy in positions + motions + mid + [border] + end:
        copy.wait_send()


def body(outer, inner, particles, occupancy, neighbours, curve_cuts):
    tiles, fields, slots = particles.shape
    listed = neighbours.shape[1]
    total = outer * inner * tiles
    reach = 2 * tiles
    half = tiles // 2
    first = lax.axis_index(("gx", "gy")) * tiles
    tile_ids = jnp.arange(tiles, dtype=jnp.int32)
    offset = (neighbours - (first + tile_ids)[:, None]) % total
    entry_ids = jnp.arange(tiles * listed, dtype=jnp.int32).reshape(tiles, listed)
    offsets = jnp.arange(1, reach + 1, dtype=jnp.int32)
    hit = offset[:, None, :] == offsets[None, :, None]
    none = tiles * listed
    inverse = none + jnp.sum(jnp.where(hit, entry_ids[:, None, :] - none, 0), axis=2)
    out_type = jax.ShapeDtypeStruct((2 * tiles, fields, slots), F32)
    vmem = pl.BlockSpec(memory_space=pltpu.VMEM)
    smem = pl.BlockSpec(memory_space=pltpu.SMEM)

    def rows(*extent):
        return pltpu.VMEM(extent + (slots,), F32)

    return pl.pallas_call(
        functools.partial(kernel, (outer, inner, tiles, listed, half)),
        out_shape=(out_type, out_type),
        in_specs=[smem, smem, smem, smem, vmem],
        out_specs=(vmem, vmem),
        scratch_shapes=[
            rows(3 * tiles, 4),
            rows(3 * tiles, 4),
            rows(3 * tiles, 4),
            rows(3 * tiles + half, 8),
            pltpu.VMEM((3 * tiles, 16, slots), BF16),
            rows(tiles, 3, slots),
            pltpu.VMEM((tiles, slots, 16), F32),
            rows(tiles, 8),
            rows(tiles * listed + 1, 8),
            rows(STEPS, 3 * tiles, 4),
            rows(2 * tiles, 4),
            rows(tiles, 4),
            rows(2 * tiles, 4),
            rows(tiles, 4),
            rows(2 * tiles, 4),
            rows(half, 4),
            rows(tiles + half, 4),
            rows(half, 4),
            rows(2 * tiles, fields),
            rows(2 * tiles, fields),
            pltpu.SemaphoreType.DMA((13,)),
            pltpu.SemaphoreType.DMA((13,)),
        ],
        compiler_params=pltpu.CompilerParams(
            collective_id=0, has_side_effects=True, vmem_limit_bytes=40 << 20
        ),
    )(neighbours, inverse, occupancy, curve_cuts, particles)


def solution(mesh):
    in_specs = (P(("gx", "gy"), None, None), P(("gx", "gy")), P(("gx", "gy"), None), P())
    out_specs = (P(("gx", "gy"), None, None), P(("gx", "gy"), None, None))
    per_device = functools.partial(body, mesh.shape["gx"], mesh.shape["gy"])
    return jax.shard_map(
        per_device, mesh=mesh, in_specs=in_specs, out_specs=out_specs, check_vma=False
    )
```

```python
import functools

import jax
import jax.numpy as jnp
from jax import lax
from jax.experimental import pallas as pl
from jax.experimental.pallas import tpu as pltpu
from jax.sharding import PartitionSpec as P

STEPS = 2
soften = 0.05
time_step = 0.5

MESH = pl.DeviceIdType.MESH
F32 = jnp.float32
BF16 = jnp.bfloat16


def split_rows(rows):
    high = rows.astype(BF16)
    rest = rows - high.astype(F32)
    middle = rest.astype(BF16)
    low = rest - middle.astype(F32)
    return jnp.concatenate(
        [high.astype(F32), low, middle.astype(F32), jnp.zeros_like(low)], axis=0
    ).astype(BF16)


def fold(terms):
    return terms[:4] + terms[4:]


def kernel(
    dims, neighbours_far, occupancy_far, cuts_far, part_far, first_out, second_out,
    first_pool, second_pool, speeds, state, terms, columns, self_act, act, react_all,
    partial, from_next, from_second_next, from_last, from_second_last,
    end_last, end_next, end_second_last, end_third_last, first_window, second_window,
    neighbours, neighbour_rows, occupancy, cuts, part, inverse_rows, inverse,
    send, recv, near,
):
    outer, inner, tiles, listed, half = dims
    pools = (first_pool, second_pool)
    size = outer * inner
    total_tiles = size * tiles
    reach = 2 * tiles
    slots = part_far.shape[2]
    zero_slot = tiles * listed
    me = lax.axis_index("gx") * inner + lax.axis_index("gy")
    first = me * tiles

    def device(distance):
        index = (me + distance + size) % size
        return (index // inner, index % inner)

    barrier = pltpu.get_barrier_semaphore()
    for distance in (-1, 1, -2, 2, -3, 3):
        pl.semaphore_signal(barrier, inc=1, device_id=device(distance), device_id_type=MESH)

    loads = [
        pltpu.make_async_copy(source, target, near.at[slot])
        for slot, (source, target) in enumerate(
            (
                (occupancy_far, occupancy),
                (part_far, part),
                (neighbours_far, neighbour_rows),
                (neighbours_far, neighbours),
                (cuts_far, cuts),
            ),
            1,
        )
    ]
    for load in loads:
        load.start()
    react_all[zero_slot] = jnp.zeros((8, slots), F32)
    inverse_copy = pltpu.make_async_copy(inverse_rows, inverse, near.at[0])

    def find_entries():
        own_id = lax.broadcasted_iota(jnp.int32, (tiles, listed), 0)
        entry_id = lax.broadcasted_iota(jnp.int32, (tiles, listed), 1)
        offset = neighbour_rows[...] - first - own_id
        offset = jnp.where(offset < 0, offset + total_tiles, offset)
        mark = own_id * listed + entry_id - zero_slot
        place = lax.broadcasted_iota(jnp.int32, (tiles, reach), 1)
        found = jnp.full((tiles, reach), zero_slot, jnp.int32)
        for distance in range(1, reach + 1):
            entry = jnp.sum(jnp.where(offset == distance, mark, 0), axis=1, keepdims=True)
            found = found + jnp.where(place == distance - 1, entry, 0)
        inverse_rows[...] = jnp.clip(found, 0, zero_slot)

    for load in loads:
        load.wait()
    lanes = lax.broadcasted_iota(jnp.int32, (1, slots), 1)
    empty = jnp.zeros((1, slots), F32)
    for tile in range(tiles):
        weight = jnp.where(lanes < occupancy[tile], 1.0, 0.0).astype(F32)
        first_pool[tile] = jnp.concatenate([part[tile, 0:3], weight], axis=0)
        speeds[tile] = jnp.concatenate([part[tile, 3:6], empty], axis=0)

    def remote(source, target, slot, distance):
        return pltpu.make_async_remote_copy(
            src_ref=source,
            dst_ref=target,
            send_sem=send.at[slot],
            recv_sem=recv.at[slot],
            device_id=device(distance),
            device_id_type=MESH,
        )

    def tile_copies(buffer, slot):
        return [
            remote(
                buffer.at[pl.ds(0, tiles)],
                buffer.at[pl.ds(tiles * distance, tiles)],
                slot + distance - 1,
                -distance,
            )
            for distance in (1, 2)
        ]

    def rows_copy(step, begin, count, target, slot, distance):
        return remote(partial.at[step, pl.ds(begin, count)], target, slot, distance)

    positions = tile_copies(first_pool, 0)
    motions = tile_copies(speeds, 2)
    mid = [
        rows_copy(0, tiles, 2 * tiles, from_last, 4, 1),
        rows_copy(0, 2 * tiles, tiles, from_second_last, 5, 2),
        rows_copy(0, 0, tiles, from_second_next, 6, -2),
        rows_copy(0, 0, 2 * tiles, from_next, 7, -1),
    ]
    border = remote(
        state.at[pl.ds(tiles - half, half)], state.at[pl.ds(3 * tiles, half)], 8, 1
    )
    end = [
        rows_copy(1, 2 * tiles + half, half, end_third_last, 9, 3),
        rows_copy(1, tiles + half, tiles + half, end_second_last, 10, 2),
        rows_copy(1, half, 2 * tiles, end_last, 11, 1),
        rows_copy(1, 0, half, end_next, 12, -1),
    ]

    def over(begin, end, function, unroll):
        def trip(tile, carry):
            function(tile)
            return carry

        lax.fori_loop(begin, end, trip, 0, unroll=unroll)

    def prepare(rows, tile):
        terms[tile] = split_rows(rows * rows[3:4])

    def pair(step, tile, source):
        rows = pools[step][source]
        dx = rows[0:1] - columns[tile, 0]
        dy = rows[1:2] - columns[tile, 1]
        dz = rows[2:3] - columns[tile, 2]
        root = lax.rsqrt(dx * dx + (dy * dy + (dz * dz + soften)))
        value = root * root * root
        high = value.astype(BF16)
        low = (value - high.astype(F32)).astype(BF16)
        return high, low

    def action_of(high, low, source):
        rows = terms[source]
        return lax.dot_general(
            jnp.concatenate([high, low], axis=1),
            jnp.concatenate([rows, rows], axis=1),
            (((1,), (1,)), ((), ())),
            preferred_element_type=F32,
        )

    def own_tile(step, tile):
        rows = pools[step][tile]
        prepare(rows, tile)
        turned = jnp.transpose(jnp.concatenate([rows, rows], axis=0))
        for axis in range(3):
            columns[tile, axis] = jnp.broadcast_to(turned[:, axis : axis + 1], (slots, slots))
        high, low = pair(step, tile, tile)
        self_act[tile] = action_of(high, low, tile)

    def main_tile(step, tile):
        own = terms[tile]
        own_terms = jnp.concatenate([own, own], axis=1)
        total = self_act[tile]
        for entry in range(listed):
            source = jnp.minimum(
                lax.rem(neighbours[tile, entry] - first + total_tiles, total_tiles),
                3 * tiles - 1,
            )
            high, low = pair(step, tile, source)
            total = total + action_of(high, low, source)
            reaction = jnp.dot(
                own_terms, jnp.concatenate([high, low], axis=0), preferred_element_type=F32
            )
            react_all[tile * listed + entry] = reaction[:8] + reaction[8:]
        turned = jnp.transpose(total)
        act[tile] = turned[:8] + turned[8:]

    def reactions_on(source):
        total = None
        for tile in range(max(0, source - reach), min(tiles, source)):
            entry = react_all[inverse[tile, source - tile - 1]]
            total = entry if total is None else total + entry
        return total

    def moved(place, speed, weight, total):
        acceleration = total[0:3] - place * total[3:4]
        speed = weight * (speed + (time_step / slots) * acceleration)
        place = weight * (place + time_step * speed)
        return place, speed

    find_entries()
    pl.semaphore_wait(barrier, 6)
    for copy in positions + motions:
        copy.start()
    inverse_copy.start()
    over(0, tiles, lambda tile: own_tile(0, tile), 4)
    for distance in (1, 2):
        positions[distance - 1].wait_recv()
        over(
            tiles * distance,
            tiles * (distance + 1),
            lambda tile: prepare(first_pool[tile], tile),
            4,
        )
    over(0, tiles, lambda tile: main_tile(0, tile), 1)
    inverse_copy.wait()

    for tile in range(2 * tiles, 3 * tiles):
        partial[0, tile] = fold(reactions_on(tile))
    mid[1].start()
    for tile in range(tiles, 2 * tiles):
        partial[0, tile] = fold(reactions_on(tile))
    mid[0].start()
    for tile in range(tiles):
        total = act[tile] if tile == 0 else act[tile] + reactions_on(tile)
        partial[0, tile] = fold(total)
    mid[2].start()
    mid[3].start()

    def first_update(tile, total):
        rows, speed = first_pool[tile], speeds[tile]
        place, speed = moved(rows[0:3], speed[0:3], rows[3:4], total)
        second_pool[tile] = jnp.concatenate([place, rows[3:4]], axis=0)
        state[tile] = jnp.concatenate([place, speed, rows[3:4], empty], axis=0)

    mid[0].wait_recv()
    mid[1].wait_recv()
    over(
        0,
        tiles,
        lambda tile: first_update(
            tile, partial[0, tile] + from_last[tile] + from_second_last[tile]
        ),
        4,
    )
    border.start()
    over(0, tiles, lambda tile: own_tile(1, tile), 4)
    motions[0].wait_recv()
    motions[1].wait_recv()
    mid[3].wait_recv()

    def next_update(tile):
        first_update(
            tiles + tile, from_next[tile] + partial[0, tiles + tile] + from_last[tiles + tile]
        )
        prepare(second_pool[tiles + tile], tiles + tile)

    over(0, tiles, next_update, 4)
    mid[2].wait_recv()

    def second_next_update(tile):
        first_update(
            2 * tiles + tile,
            from_second_next[tile] + from_next[tiles + tile] + partial[0, 2 * tiles + tile],
        )
        prepare(second_pool[2 * tiles + tile], 2 * tiles + tile)

    over(0, tiles, second_next_update, 4)
    over(0, tiles, lambda tile: main_tile(1, tile), 1)

    for tile in range(2 * tiles, 3 * tiles):
        partial[1, tile] = fold(reactions_on(tile))
    end[0].start()
    for tile in range(tiles, 2 * tiles):
        partial[1, tile] = fold(reactions_on(tile))
    end[1].start()
    for tile in range(tiles):
        total = act[tile] if tile == 0 else act[tile] + reactions_on(tile)
        partial[1, tile] = fold(total)
    end[2].start()
    end[3].start()

    border.wait_recv()
    for tile in range(half):
        first_window[tile] = state[3 * tiles + tile, 0:6]
    for tile in range(tiles + half):
        first_window[half + tile] = state[tile, 0:6]

    def place_slots(step, window, out):
        begin = cuts[step, me] - (first - half)
        following = cuts[step, jnp.minimum(me + 1, size - 1)]
        count = jnp.where(me + 1 < size, following, total_tiles) - cuts[step, me]
        for slot in range(2 * tiles):
            rows = window[jnp.clip(begin + slot, 0, 2 * tiles - 1)]
            out[:, slot, :] = jnp.where(slot < count, rows, 0.0)

    place_slots(0, first_window, first_out)

    def second_update(tile, slot, total):
        rows = state[tile]
        place, speed = moved(rows[0:3], rows[3:6], rows[6:7], total)
        second_window[slot] = jnp.concatenate([place, speed], axis=0)

    end[2].wait_recv()
    end[1].wait_recv()
    for tile in range(tiles):
        second_update(
            tile,
            half + tile,
            partial[1, tile] + end_last[half + tile] + end_second_last[half + tile],
        )
    end[3].wait_recv()
    for tile in range(half):
        second_update(
            tiles + tile,
            half + tiles + tile,
            end_next[tile] + partial[1, tiles + tile] + end_last[tiles + half + tile],
        )
    end[0].wait_recv()
    for tile in range(half):
        second_update(
            3 * tiles + tile, tile, end_last[tile] + end_second_last[tile] + end_third_last[tile]
        )
    place_slots(1, second_window, second_out)
    for copy in positions + motions + mid + [border] + end:
        copy.wait_send()


def body(outer, inner, particles, occupancy, neighbours, curve_cuts):
    tiles, fields, slots = particles.shape
    listed = neighbours.shape[1]
    half = tiles // 2
    out_type = jax.ShapeDtypeStruct((fields, 2 * tiles, slots), F32)
    vmem = pl.BlockSpec(memory_space=pltpu.VMEM)
    far = pl.BlockSpec(memory_space=pltpu.MemorySpace.HBM)

    def held(*extent):
        return pltpu.VMEM(extent + (slots,), F32)

    outputs = pl.pallas_call(
        functools.partial(kernel, (outer, inner, tiles, listed, half)),
        out_shape=(out_type, out_type),
        in_specs=[far] * 4,
        out_specs=(vmem, vmem),
        scratch_shapes=[
            held(3 * tiles, 4),
            held(3 * tiles, 4),
            held(3 * tiles, 4),
            held(3 * tiles + half, 8),
            pltpu.VMEM((3 * tiles, 16, slots), BF16),
            held(tiles, 3, slots),
            pltpu.VMEM((tiles, slots, 16), F32),
            held(tiles, 8),
            held(tiles * listed + 1, 8),
            held(STEPS, 3 * tiles, 4),
            held(2 * tiles, 4),
            held(tiles, 4),
            held(2 * tiles, 4),
            held(tiles, 4),
            held(2 * tiles, 4),
            held(half, 4),
            held(tiles + half, 4),
            held(half, 4),
            held(2 * tiles, fields),
            held(2 * tiles, fields),
            pltpu.SMEM(neighbours.shape, jnp.int32),
            pltpu.VMEM(neighbours.shape, jnp.int32),
            pltpu.SMEM(occupancy.shape, jnp.int32),
            pltpu.SMEM(curve_cuts.shape, jnp.int32),
            pltpu.VMEM(particles.shape, F32),
            pltpu.VMEM((tiles, 2 * tiles), jnp.int32),
            pltpu.SMEM((tiles, 2 * tiles), jnp.int32),
            pltpu.SemaphoreType.DMA((13,)),
            pltpu.SemaphoreType.DMA((13,)),
            pltpu.SemaphoreType.DMA((6,)),
        ],
        compiler_params=pltpu.CompilerParams(
            collective_id=0, has_side_effects=True, vmem_limit_bytes=40 << 20
        ),
    )(
        *(
            pltpu.with_memory_space_constraint(operand, pltpu.MemorySpace.HBM)
            for operand in (neighbours, occupancy, curve_cuts, particles)
        )
    )
    return tuple(jnp.transpose(rows, (1, 0, 2)) for rows in outputs)


def solution(mesh):
    in_specs = (P(("gx", "gy"), None, None), P(("gx", "gy")), P(("gx", "gy"), None), P())
    out_specs = (P(("gx", "gy"), None, None), P(("gx", "gy"), None, None))
    per_device = functools.partial(body, mesh.shape["gx"], mesh.shape["gy"])
    return jax.shard_map(
        per_device, mesh=mesh, in_specs=in_specs, out_specs=out_specs, check_vma=False
    )
```
